32 devices in a mesh: mem: 4 (over y, x), band: 8 (over z, core).
Axes of the slice: x: 2, y: 2, z: 4, core: 2. Of those that a mesh axis runs over, the one named last changes fastest.
Arguments:
- control: bfloat16 [32, 512, 1024], P('mem', 'band'), may hold values from -6 to 6
- lon_corr: bfloat16 [1024, 1024], replicated, may hold values from -0.1875 to 0.1875
- lat_corr: bfloat16 [512, 512], replicated, may hold values from -0.25 to 0.25
- members_fine: bfloat16 [32, 2048, 2048], P('mem', 'band'), may hold values from -0.8984375 to 0.8984375
- innovation: float32 [2048, 2048], P('band'), may hold values from -6 to 6
- obs_error: float32 [2048, 2048], P('band'), may hold values from 0.4 to 2
- tile_rows: int32 [8], replicated, may hold values from 1 to 256, 1024 in all
- obs_count: int32 [8], replicated, may hold values from 131072 to 524288
Outputs:
- gradient: float32 [32, 512, 1024], P('mem', 'band')
- increment: float32 [2048, 2048], P('band')
The draws below stay inside these ranges and needn't reach their ends.
Inputs may be any that keep to these rules, and one draw needn't show every extreme that they name: `tile_rows`: the entries sum to 1024 and the largest is exactly 256.
All inputs are finite; a program needn't handle non-finite values.
Results may differ from the reference program's by a relative error of at most 0.0087.
Values may be sent and summed in bfloat16 or wider, within the bound.
No kernel may reach another device: no remote copies, remote signals or barrier semaphores. Data moves between devices by JAX's collectives and lax.ppermute only.
A program may use at most 128 MiB of HBM per device.

```python
import math
import jax
import jax.numpy as jnp
import numpy as np
from jax import lax

CLAT = 512
CLON = 1024
FLAT = 1024
FLON = 2048
MEMBERS = 32
FCAP = 256
N_BAND = 8


def with_ends(drawn, stream_key, least, largest):
    place = [jax.random.randint(jax.random.fold_in(stream_key, axis), (), 0, length) for axis, length in enumerate(drawn.shape)]
    main_axis = drawn.shape.index(max(drawn.shape))
    neighbour = place[:main_axis] + [(place[main_axis] + 1) % drawn.shape[main_axis]] + place[main_axis + 1:]
    return drawn.at[tuple(place)].set(least).at[tuple(neighbour)].set(largest)


def steps_of(key, shape, cuts, low, largest):
    level, own = 1.0, jax.random.fold_in(key, 6)
    for dim, blocks in cuts:
        steps = jnp.exp(jax.random.uniform(jax.random.fold_in(own, dim), (blocks,), jnp.float32, low / len(cuts), largest / len(cuts)))
        level = level * jnp.repeat(steps, shape[dim] // blocks).reshape([-1 if axis == dim else 1 for axis in range(len(shape))])
    return level


def split_up(amount, total, reach, skew):
    loads = [(1 << 20) // math.isqrt(standing ** skew) + 1 for standing in range(2, amount + 1)]
    spare, given = total - reach - (amount - 1), [1] * (amount - 1)
    while spare > 0:
        movable = [i for i in range(amount - 1) if given[i] < reach]
        pool, budget = sum([loads[i] for i in movable]), spare
        for i in movable:
            addition = min(reach - given[i], max(1, budget * loads[i] // pool), spare)
            given[i] = given[i] + addition
            spare = spare - addition
    return np.array([reach] + given)


def uneven(rng, count, total, limit, slope):
    if count == 2:
        one = jax.random.randint(rng, (), max(1, total - limit), min(limit, total - 1) + 1)
        return jnp.stack([one, total - one])
    lengths = jnp.asarray(split_up(count, total, limit, slope), jnp.int32)
    pairs = (count - 1) // 2
    giver, receiver = lengths[1:1 + 2 * pairs:2], lengths[2:2 + 2 * pairs:2]
    room = jnp.minimum(giver - 1, limit - receiver)
    moved = jax.random.randint(jax.random.fold_in(rng, 1), (pairs,), 0, 1 << 20) % (room + 1)
    lengths = lengths.at[1:1 + 2 * pairs:2].set(giver - moved).at[2:2 + 2 * pairs:2].set(receiver + moved)
    return lengths[jax.random.permutation(jax.random.fold_in(rng, 2), count)]


def normal_values(stream_key, shape, scale, most, shards=(), kind=jnp.bfloat16):
    drawn = scale * jax.random.normal(stream_key, shape, jnp.float32)
    if shards:
        drawn = drawn * steps_of(stream_key, shape, shards, -0.22, 0.18)
    return jnp.clip(drawn, -most, most).astype(kind)


def setup_inputs(seed: int = 0) -> dict:
    seeds = jax.random.split(jax.random.key(seed), 9)
    control = normal_values(seeds[0], (MEMBERS, CLAT, CLON), 1.0, 6.0, ((0, 4), (1, 8)))
    lon_corr = normal_values(seeds[1], (CLON, CLON), CLON ** -0.5, 0.1875)
    lat_corr = normal_values(seeds[2], (CLAT, CLAT), CLAT ** -0.5, 0.25)
    members_fine = normal_values(seeds[3], (MEMBERS, N_BAND * FCAP, FLON), 0.15, 0.8984375, ((0, 4), (1, 8)))
    innovation = normal_values(seeds[4], (N_BAND * FCAP, FLON), 1.0, 6.0, ((0, 8),), jnp.float32)
    obs_error = jnp.clip(jnp.exp(math.log(2.0) - 1.609438 * jax.random.uniform(seeds[5], (N_BAND * FCAP, FLON), jnp.float32) ** steps_of(seeds[5], (N_BAND * FCAP, FLON), ((0, 8),), -0.2, 0.2)), 0.4, 2.0)
    tile_rows = uneven(seeds[6], N_BAND, FLAT, FCAP, 2).astype(jnp.int32)
    obs_count = with_ends(jax.random.randint(seeds[7], (N_BAND,), FCAP * FLON // 4, FCAP * FLON + 1), jax.random.fold_in(seeds[7], 1), FCAP * FLON // 4, FCAP * FLON).astype(jnp.int32)
    return {"control": control, "lon_corr": lon_corr, "lat_corr": lat_corr, "members_fine": members_fine, "innovation": innovation, "obs_error": obs_error, "tile_rows": tile_rows, "obs_count": obs_count}


huber_edge = 1.5


def rounded(values):
    return lax.optimization_barrier(values.astype(jnp.bfloat16)).astype(jnp.float32)


def reference(control, lon_corr, lat_corr, members_fine, innovation, obs_error, tile_rows, obs_count):
    slot_total = N_BAND * FCAP
    slot = jnp.arange(slot_total, dtype=jnp.int32)
    owner = slot // FCAP
    inner = slot % FCAP
    starts = jnp.cumsum(tile_rows) - tile_rows
    valid = inner < tile_rows[owner]
    fine_row = jnp.minimum(starts[owner] + inner, FLAT - 1).astype(jnp.int32)
    position = fine_row.astype(jnp.float32) * (CLAT - 1) / (FLAT - 1)
    lower = ((fine_row * (CLAT - 1)) // (FLAT - 1)).astype(jnp.int32)
    upper = jnp.minimum(lower + 1, CLAT - 1).astype(jnp.int32)
    low_w = rounded(jnp.where(valid, 1.0 - jnp.abs(position - lower.astype(jnp.float32)), 0.0).astype(jnp.float32))
    high_w = rounded(jnp.where(valid, jnp.maximum(0.0, 1.0 - jnp.abs(position - (lower + 1).astype(jnp.float32))), 0.0).astype(jnp.float32))
    corr_float = lat_corr.astype(jnp.float32)
    lat_op = (low_w[:, None] * corr_float[lower] + high_w[:, None] * corr_float[upper]).astype(jnp.bfloat16)
    column = jnp.arange(FLON, dtype=jnp.int32)
    lon_pos = column.astype(jnp.float32) * (CLON - 1) / (FLON - 1)
    left = ((column * (CLON - 1)) // (FLON - 1)).astype(jnp.int32)
    right = jnp.minimum(left + 1, CLON - 1).astype(jnp.int32)
    left_w = rounded(1.0 - jnp.abs(lon_pos - left.astype(jnp.float32)))
    right_w = rounded(jnp.maximum(0.0, 1.0 - jnp.abs(lon_pos - (left + 1).astype(jnp.float32))))

    def forward(total, pair):
        weights, perturb = pair
        mixed = jnp.dot(weights, lon_corr, preferred_element_type=jnp.float32).astype(jnp.bfloat16)
        lat_fine = rounded(jnp.dot(lat_op, mixed, preferred_element_type=jnp.float32))
        fine = lat_fine[:, left] * left_w[None, :] + lat_fine[:, right] * right_w[None, :]
        return total + perturb.astype(jnp.float32) * fine, None

    increment = lax.scan(forward, jnp.zeros((slot_total, FLON), jnp.float32), (control, members_fine))[0]
    observed = valid[:, None] & (inner[:, None] * FLON + column[None, :] < obs_count[owner][:, None])
    scaled = (increment - innovation) / obs_error
    weight = huber_edge / jnp.maximum(jnp.abs(scaled), huber_edge)
    pull = jnp.where(observed, weight * scaled / obs_error, 0.0).astype(jnp.float32)

    def adjoint(perturb):
        fine_grad = rounded(perturb.astype(jnp.float32) * pull)
        lon_back = jnp.zeros((slot_total, CLON), jnp.float32)
        lon_back = lon_back.at[:, left].add(fine_grad * left_w[None, :]).at[:, right].add(fine_grad * right_w[None, :])
        lon_back = lon_back.astype(jnp.bfloat16)
        lat_back = jnp.dot(lat_op.T, lon_back, preferred_element_type=jnp.float32).astype(jnp.bfloat16)
        return jnp.dot(lat_back, lon_corr.T, preferred_element_type=jnp.float32)

    gradient = lax.map(adjoint, members_fine)
    return gradient, increment
```

```python
import functools

import jax
import jax.numpy as jnp
import numpy as np
from jax import lax
from jax.experimental import pallas as pl
from jax.experimental.pallas import tpu as pltpu
from jax.sharding import PartitionSpec as P

FLAT = 1024
CHUNKS = 4
EDGE = 128

huber_edge = 1.5


def f32(values):
    return values.astype(jnp.float32)


def ring_order(chips):
    up = list(range(0, chips, 2))
    down = list(range(1, chips, 2))[::-1]
    return up + down


def ring_tables(chips):
    order = ring_order(chips)
    place = {chip: at for at, chip in enumerate(order)}
    steps = [0]
    for distance in range(1, chips // 2):
        steps += [-distance, distance]
    steps += [chips // 2]
    table = np.array(
        [[order[(place[chip] + step) % chips] for step in steps] for chip in range(chips)], np.int32
    )
    ahead = []
    for chip in range(chips):
        target = order[(place[chip] + 1) % chips]
        ahead += [(2 * chip + core, 2 * target + core) for core in range(2)]
    back = [(there, here) for here, there in ahead]
    return table, ahead, back


def dot(left, right):
    return jnp.dot(left, right, preferred_element_type=jnp.float32)


def forward_kernel(has_prev, overlap, x_ref, y_ref, op_ref, interp_ref, mf_ref, *rest):
    if has_prev:
        prev_ref, lat_ref, part_ref, acc_ref = rest
    else:
        lat_ref, part_ref, acc_ref = rest
    member = pl.program_id(0)
    chips, _, rows, width = x_ref.shape
    half = chips * rows
    lat = dot(op_ref[:, :half], x_ref[...].reshape(half, width))
    lat = lat + dot(op_ref[:, half:], y_ref[...].reshape(half, width))
    lat = lat.astype(jnp.bfloat16)
    lat_ref[0] = lat
    if has_prev:
        start = prev_ref.shape[2] - overlap
        fine = dot(prev_ref[0, :, start:], interp_ref[:overlap, :]) + dot(lat, interp_ref[overlap:, :])
    else:
        fine = dot(lat, interp_ref[...])
    term = f32(mf_ref[0]) * fine

    @pl.when(member == 0)
    def _():
        acc_ref[...] = term

    @pl.when(member > 0)
    def _():
        acc_ref[...] += term

    @pl.when(member == pl.num_programs(0) - 1)
    def _():
        part_ref[...] = acc_ref[...].astype(jnp.bfloat16)


def forward_chunk(chunk, x, y, op, interp, members, prev, overlap, fine_width):
    chips, count, rows, width = x.shape
    capacity = op.shape[0]
    in_specs = [
        pl.BlockSpec((chips, 1, rows, width), lambda m: (0, m, 0, 0)),
        pl.BlockSpec((chips, 1, rows, width), lambda m: (0, m, 0, 0)),
        pl.BlockSpec(op.shape, lambda m: (0, 0)),
        pl.BlockSpec(interp.shape, lambda m: (0, 0)),
        pl.BlockSpec((1, capacity, fine_width), lambda m: (m, 0, chunk)),
    ]
    operands = [x, y, op, interp, members]
    if prev is not None:
        in_specs.append(pl.BlockSpec((1, capacity, prev.shape[2]), lambda m: (m, 0, 0)))
        operands.append(prev)
    flops = 2 * count * capacity * (op.shape[1] * width + interp.shape[0] * fine_width)
    moved = 2 * (2 * x.size + op.size + interp.size + count * capacity * (fine_width + 2 * width))
    return pl.pallas_call(
        functools.partial(forward_kernel, prev is not None, overlap),
        grid=(count,),
        in_specs=in_specs,
        out_specs=[
            pl.BlockSpec((1, capacity, width), lambda m: (m, 0, 0)),
            pl.BlockSpec((capacity, fine_width), lambda m: (0, 0)),
        ],
        out_shape=[
            jax.ShapeDtypeStruct((count, capacity, width), jnp.bfloat16),
            jax.ShapeDtypeStruct((capacity, fine_width), jnp.bfloat16),
        ],
        scratch_shapes=[pltpu.VMEM((capacity, fine_width), jnp.float32)],
        cost_estimate=pl.CostEstimate(flops=flops, bytes_accessed=moved, transcendentals=0),
        name=f"forward{chunk}",
    )(*operands)


def pull_kernel(first, last, chunk, split, scal_ref, own_ref, far_ref, innov_ref, err_ref, mf_ref, interp_ref, *rest):
    rest = list(rest)
    carry_in = None if first else rest.pop(0)
    if not first:
        rest.pop(0)
    inc_ref, send_ref = rest[:2]
    carry_out = None if last else rest[2]
    pull_ref = rest[-1]
    member = pl.program_id(0)
    capacity, fine_width = pull_ref.shape

    @pl.when(member == 0)
    def _():
        total = f32(own_ref[...]) + f32(far_ref[...])
        inc_ref[...] = total
        spread = err_ref[...]
        scaled = (total - innov_ref[...]) / spread
        weight = huber_edge / jnp.maximum(jnp.abs(scaled), huber_edge)
        slot = lax.broadcasted_iota(jnp.int32, (capacity, fine_width), 0)
        column = lax.broadcasted_iota(jnp.int32, (capacity, fine_width), 1) + chunk * fine_width
        observed = (slot < scal_ref[0]) & (slot * scal_ref[2] + column < scal_ref[1])
        pull_ref[...] = jnp.where(observed, weight * scaled / spread, 0.0)

    grad = (f32(mf_ref[0]) * pull_ref[...]).astype(jnp.bfloat16)
    back = dot(grad, interp_ref[...])
    if first:
        send_ref[0] = back[:, :split].astype(jnp.bfloat16)
    else:
        joined = back[:, :split] + f32(carry_in[0])
        send_ref[0, :, :split] = joined.astype(jnp.bfloat16)
    if last:
        send_ref[0, :, split:] = back[:, split:].astype(jnp.bfloat16)
    else:
        carry_out[0] = back[:, split:].astype(jnp.bfloat16)


def pull_chunk(chunk, chunks, scal, own, far, innovation, obs_error, members, interp, split, carry, inc):
    count, capacity, fine_lon = members.shape
    fine_width = own.shape[1]
    window = interp.shape[1]
    first, last = chunk == 0, chunk == chunks - 1
    sent = window if last else split
    in_specs = [
        pl.BlockSpec(memory_space=pltpu.SMEM),
        pl.BlockSpec((capacity, fine_width), lambda m: (0, 0)),
        pl.BlockSpec((capacity, fine_width), lambda m: (0, 0)),
        pl.BlockSpec((capacity, fine_width), lambda m: (0, chunk)),
        pl.BlockSpec((capacity, fine_width), lambda m: (0, chunk)),
        pl.BlockSpec((1, capacity, fine_width), lambda m: (m, 0, chunk)),
        pl.BlockSpec(interp.shape, lambda m: (0, 0)),
    ]
    operands = [scal, own, far, innovation, obs_error, members, interp]
    aliases = {}
    if not first:
        in_specs.append(pl.BlockSpec((1, capacity, carry.shape[2]), lambda m: (m, 0, 0)))
        in_specs.append(pl.BlockSpec(memory_space=pl.ANY))
        operands += [carry, inc]
        aliases = {len(operands) - 1: 0}
    out_specs = [
        pl.BlockSpec((capacity, fine_width), lambda m: (0, chunk)),
        pl.BlockSpec((1, capacity, sent), lambda m: (m, 0, 0)),
    ]
    out_shape = [
        jax.ShapeDtypeStruct((capacity, fine_lon), jnp.float32),
        jax.ShapeDtypeStruct((count, capacity, sent), jnp.bfloat16),
    ]
    if not last:
        out_specs.append(pl.BlockSpec((1, capacity, window - split), lambda m: (m, 0, 0)))
        out_shape.append(jax.ShapeDtypeStruct((count, capacity, window - split), jnp.bfloat16))
    flops = 2 * count * capacity * fine_width * (window + 1)
    moved = 2 * count * capacity * (fine_width + window) + 18 * capacity * fine_width
    return pl.pallas_call(
        functools.partial(pull_kernel, first, last, chunk, split),
        grid=(count,),
        in_specs=in_specs,
        out_specs=out_specs,
        out_shape=out_shape,
        scratch_shapes=[pltpu.VMEM((capacity, fine_width), jnp.float32)],
        input_output_aliases=aliases,
        cost_estimate=pl.CostEstimate(flops=flops, bytes_accessed=moved, transcendentals=0),
        name=f"pull{chunk}",
    )(*operands)


def back_kernel(own_ref, far_ref, op_ref, *out_refs):
    capacity = own_ref.shape[1]
    rows = out_refs[0].shape[1]
    total = dot(op_ref[:, :capacity], own_ref[0]) + dot(op_ref[:, capacity:], far_ref[0])
    for at, out_ref in enumerate(out_refs):
        out_ref[0] = total[at * rows : (at + 1) * rows].astype(jnp.bfloat16)


def back_chunk(chunk, own, far, op, chips):
    count, capacity, width = own.shape
    rows = op.shape[0] // chips
    return pl.pallas_call(
        back_kernel,
        grid=(count,),
        in_specs=[
            pl.BlockSpec((1, capacity, width), lambda m: (m, 0, 0)),
            pl.BlockSpec((1, capacity, width), lambda m: (m, 0, 0)),
            pl.BlockSpec(op.shape, lambda m: (0, 0)),
        ],
        out_specs=[pl.BlockSpec((1, rows, width), lambda m: (m, 0, 0))] * chips,
        out_shape=[jax.ShapeDtypeStruct((count, rows, width), jnp.bfloat16)] * chips,
        cost_estimate=pl.CostEstimate(
            flops=2 * count * op.size * width,
            bytes_accessed=2 * (2 * own.size + op.size + count * op.shape[0] * width),
            transcendentals=0,
        ),
        name=f"back{chunk}",
    )(own, far, op)


def interp_window(fine_start, fine_width, low, high, fine_lon, coarse_lon, coarse_axis):
    shape = (high - low, fine_width) if coarse_axis == 0 else (fine_width, high - low)
    column = lax.broadcasted_iota(jnp.int32, shape, 1 - coarse_axis) + fine_start
    index = lax.broadcasted_iota(jnp.int32, shape, coarse_axis) + low
    place = f32(column) * (coarse_lon - 1) / (fine_lon - 1)
    return jnp.maximum(0.0, 1.0 - jnp.abs(place - f32(index))).astype(jnp.bfloat16)


def shards(mesh_shape, control, lon_corr, lat_corr, members, innovation, obs_error, tile_rows, obs_count):
    bands, groups = mesh_shape["band"], mesh_shape["mem"]
    chips = bands // 2
    count, rows, coarse_lon = control.shape
    coarse_lat = lat_corr.shape[0]
    capacity, fine_lon = members.shape[1], members.shape[2]
    chunks = CHUNKS
    fine_width = fine_lon // chunks
    coarse_width = coarse_lon // chunks
    table, ahead, back = ring_tables(chips)
    partner = [(band, band ^ 1) for band in range(bands)]
    halves = count // 2

    band = lax.axis_index("band")
    chip, core = band // 2, band % 2
    move = lambda values, perm: lax.ppermute(values, "band", perm)

    gather_cuts = [0] + [min(coarse_lon, coarse_width * (c + 1) + EDGE) for c in range(chunks)]
    scatter_cuts = [0] + [coarse_width * (c + 1) - EDGE for c in range(chunks - 1)] + [coarse_lon]

    flat = control.reshape(count * rows, coarse_lon)
    mine, theirs = [], []
    for c in range(chunks):
        low, high = gather_cuts[c], gather_cuts[c + 1]
        block = dot(flat, lon_corr[:, low:high]).astype(jnp.bfloat16).reshape(count, rows, high - low)
        parts = [block]
        left = right = block
        for _ in range(chips // 2 - 1):
            left, right = move(left, ahead), move(right, back)
            parts += [left, right]
        far = [move(left[:halves], ahead), move(right[halves:], back)]
        parts.append(jnp.concatenate(far, axis=0))
        stacked = jnp.stack(parts)
        mine.append(stacked)
        theirs.append(move(stacked, partner))

    tiles = jnp.arange(bands, dtype=jnp.int32)
    pair = jnp.stack([band, band ^ 1])
    pick = pair[:, None] == tiles[None, :]
    pair_rows = jnp.sum(jnp.where(pick, tile_rows[None, :], 0), axis=1)
    pair_start = jnp.sum(jnp.where(tiles[None, :] < pair[:, None], tile_rows[None, :], 0), axis=1)
    count_here = jnp.sum(jnp.where(tiles == band, obs_count, 0))
    scal = jnp.stack([pair_rows[0], count_here, jnp.int32(fine_lon)]).astype(jnp.int32)
    inner = jnp.arange(capacity, dtype=jnp.int32)
    live = (inner[None, :] < pair_rows[:, None]).reshape(1, -1)
    fine_row = jnp.minimum(pair_start[:, None] + inner[None, :], FLAT - 1).reshape(1, -1)
    place = f32(fine_row) * (coarse_lat - 1) / (FLAT - 1)
    index = lax.broadcasted_iota(jnp.int32, (coarse_lat, 2 * capacity), 0)
    lat_interp = jnp.where(live, jnp.maximum(0.0, 1.0 - jnp.abs(place - f32(index))), 0.0)
    lat_op = lax.dot_general(
        lat_corr, lat_interp.astype(jnp.bfloat16), (((0,), (0,)), ((), ())), preferred_element_type=jnp.float32
    ).astype(jnp.bfloat16)
    lat_op = lat_op.reshape(chips, 2, rows, 2 * capacity)
    near = lax.dynamic_index_in_dim(lat_op, core, 1, keepdims=False)
    other = lax.dynamic_index_in_dim(lat_op, 1 - core, 1, keepdims=False)
    ring = jnp.asarray(table)[chip]
    near = jnp.concatenate([lax.dynamic_index_in_dim(near, ring[i], 0, keepdims=False) for i in range(chips)])
    other = jnp.concatenate([lax.dynamic_index_in_dim(other, ring[i], 0, keepdims=False) for i in range(chips)])
    op_forward = jnp.concatenate([near[:, :capacity], other[:, :capacity]]).T
    op_back = near
    op_forward, op_back = lax.optimization_barrier((op_forward, op_back))

    prev = carry = inc = gradient = None
    for c in range(chunks):
        low = 0 if c == 0 else coarse_width * c - EDGE
        high = gather_cuts[c + 1]
        overlap = 0 if c == 0 else gather_cuts[c] - low
        make = functools.partial(interp_window, c * fine_width, fine_width, low, high, fine_lon, coarse_lon)
        interp, interp_back = lax.optimization_barrier((make(0), make(1)))
        prev, partial = forward_chunk(
            c, mine[c], theirs[c], op_forward, interp, members, prev, overlap, fine_width
        )
        bits = groups.bit_length() - 1
        far = jnp.zeros_like(partial)
        for bit in range(bits):
            perm = [(group, group ^ (1 << bit)) for group in range(groups)]
            far = lax.ppermute(partial, "mem", perm)
            if bit < bits - 1:
                partial = (f32(partial) + f32(far)).astype(jnp.bfloat16)
        split = scatter_cuts[c + 1] - low if c < chunks - 1 else (overlap if c else high)
        outs = pull_chunk(
            c, chunks, scal, partial, far, innovation, obs_error, members, interp_back, split, carry, inc
        )
        inc, sent = outs[0], outs[1]
        carry = outs[2] if c < chunks - 1 else None
        blocks = back_chunk(c, sent, move(sent, partner), op_back, chips)
        own, opposite = blocks[0], blocks[-1]
        behind = {d: blocks[2 * d - 1] for d in range(1, chips // 2)}
        front = {d: blocks[2 * d] for d in range(1, chips // 2)}
        up, down = move(opposite[:halves], ahead), move(opposite[halves:], back)
        for d in range(chips // 2 - 1, 0, -1):
            if up.shape[0] == halves:
                going = jnp.concatenate([(f32(front[d][:halves]) + f32(up)).astype(jnp.bfloat16), front[d][halves:]])
                coming = jnp.concatenate([behind[d][:halves], (f32(behind[d][halves:]) + f32(down)).astype(jnp.bfloat16)])
            else:
                going = (f32(front[d]) + f32(up)).astype(jnp.bfloat16)
                coming = (f32(behind[d]) + f32(down)).astype(jnp.bfloat16)
            up, down = move(going, ahead), move(coming, back)
        summed = (f32(own) + f32(up) + f32(down)).astype(jnp.bfloat16)
        window = lon_corr[:, scatter_cuts[c] : scatter_cuts[c + 1]]
        term = lax.dot_general(
            summed.reshape(count * rows, -1), window, (((1,), (1,)), ((), ())), preferred_element_type=jnp.float32
        )
        gradient = term if gradient is None else gradient + term
    return gradient.reshape(count, rows, coarse_lon), inc


def solution(mesh):
    placed = (
        P("mem", "band", None),
        P(),
        P(),
        P("mem", "band", None),
        P("band", None),
        P("band", None),
        P(),
        P(),
    )
    return jax.shard_map(
        functools.partial(shards, dict(mesh.shape)),
        mesh=mesh,
        in_specs=placed,
        out_specs=(P("mem", "band", None), P("band", None)),
        check_vma=False,
    )
```
